256 devices in a mesh: pairs: 32 (over z, x), sect: 8 (over y, core).
Axes of the slice: x: 4, y: 4, z: 8, core: 2. Of those that a mesh axis runs over, the one named last changes fastest.
Arguments:
- wavefunction: bfloat16 [8192, 1024], P('sect'), may hold values from -6 to 6
- left_normal: bfloat16 [64, 16, 512, 512], P('pairs', 'sect'), may hold values from -0.03125 to 0.03125
- left_comp: bfloat16 [64, 16, 512, 512], P('pairs', 'sect'), may hold values from -0.03125 to 0.03125
- right_comp: bfloat16 [64, 2, 512, 512], P('pairs'), may hold values from -0.25 to 0.25
- right_normal: bfloat16 [64, 2, 512, 512], P('pairs'), may hold values from -0.25 to 0.25
- pair_shift: int32 [64], P('pairs'), may hold values from 0 to 1
- pair_count: int32 [32], P('pairs'), may hold values from 1 to 2, as said below
- sector_rows: int32 [16], P('sect'), may hold values from 128 to 512, as said below
Outputs:
- sigma: bfloat16 [8192, 1024], P(('sect', 'pairs'))
The draws below stay inside these ranges and needn't reach their ends.
Inputs may be any that keep to these rules, and one draw needn't show every extreme that they name: Index i of pairs holds pair slots i * 2 to (i + 1) * 2 - 1, of which the first pair_count[i] are live; some index has all 2 live. Rows of sector s at or beyond sector_rows[s] are padding; some sector uses all 512 rows.
All inputs are finite; a program needn't handle non-finite values.
Results may differ from the reference program's by a relative error of at most 0.005.
Values may be sent and summed in bfloat16 or wider, within the bound.
No kernel may reach another device: no remote copies, remote signals or barrier semaphores. Data moves between devices by JAX's collectives and lax.ppermute only.
A program may use at most 128 MiB of HBM per device.

```python
import jax
import jax.numpy as jnp
from jax import lax

B = 512
KB = 512
KS = 2
PAIR_DEV = 2
SECTORS = 16
PAIRS = 64
K = 1024
N_PAIRS = 32


def draw_pair_count(key, part):
    key_counts, key_chosen = jax.random.split(key)
    counts = jax.random.randint(key_counts, (N_PAIRS,), 1, PAIR_DEV + 1)
    chosen_index = jax.random.randint(key_chosen, (), 0, N_PAIRS)
    return jnp.where(jnp.arange(N_PAIRS) == chosen_index, PAIR_DEV, counts).astype(jnp.int32)


def draw_sector_rows(key, part):
    key_rows, key_chosen = jax.random.split(key)
    counts = jax.random.randint(key_rows, (SECTORS,), B // 4, B + 1)
    chosen_index = jax.random.randint(key_chosen, (), 0, SECTORS)
    return jnp.where(jnp.arange(SECTORS) == chosen_index, B, counts).astype(jnp.int32)


def set_ends(values, rng, low, top_value):
    longest = values.shape.index(max(values.shape))
    spots = []
    for shift in (0, 1):
        where = [jax.random.randint(jax.random.fold_in(rng, axis), (), 0, length) for axis, length in enumerate(values.shape)]
        where[longest] = (where[longest] + shift) % values.shape[longest]
        spots.append(tuple(where))
    return values.at[spots[0]].set(low).at[spots[1]].set(top_value)


def block_levels(stream_key, dims, cuts, smallest, high):
    gain, own = 1.0, jax.random.fold_in(stream_key, 6)
    for dim, blocks in cuts:
        draws = jnp.exp(jax.random.uniform(jax.random.fold_in(own, dim), (blocks,), jnp.float32, smallest / len(cuts), high / len(cuts)))
        gain = gain * jnp.repeat(draws, dims[dim] // blocks).reshape([-1 if axis == dim else 1 for axis in range(len(dims))])
    return gain


def centred(stream_key, dims, width, bound, shards=(), held_as=jnp.bfloat16):
    values = width * jax.random.normal(stream_key, dims, jnp.float32)
    if shards:
        values = values * block_levels(stream_key, dims, shards, -0.22, 0.18)
    return jnp.clip(values, -bound, bound).astype(held_as)


def setup_inputs(seed: int = 0) -> dict:
    key_list = jax.random.split(jax.random.key(seed), 9)
    return {
        "wavefunction": centred(key_list[0], (SECTORS * B, K), 1.0, 6.0, ((0, 8),)),
        "left_normal": centred(key_list[1], (PAIRS, SECTORS, B, B), (B * PAIRS) ** -0.5, 0.03125, ((0, 32), (1, 8))),
        "left_comp": centred(key_list[2], (PAIRS, SECTORS, B, B), (B * PAIRS) ** -0.5, 0.03125, ((0, 32), (1, 8))),
        "right_comp": centred(key_list[3], (PAIRS, KS, KB, KB), KB ** -0.5, 0.25, ((0, 32),)),
        "right_normal": centred(key_list[4], (PAIRS, KS, KB, KB), KB ** -0.5, 0.25, ((0, 32),)),
        "pair_shift": set_ends(jax.random.randint(key_list[5], (PAIRS,), 0, KS), jax.random.fold_in(key_list[5], 1), 0, KS - 1).astype(jnp.int32),
        "pair_count": draw_pair_count(jax.random.fold_in(key_list[8], 71), 0),
        "sector_rows": draw_sector_rows(jax.random.fold_in(key_list[8], 71), 0),
    }


def reference(wavefunction, left_normal, left_comp, right_comp, right_normal, pair_shift, pair_count, sector_rows):
    row_ids = jnp.arange(B, dtype=jnp.int32)
    row_keep = row_ids[None, :] < sector_rows[:, None]
    blocked = wavefunction.reshape(SECTORS, B, K)
    masked = jnp.where(row_keep[:, :, None], blocked, jnp.zeros((), jnp.bfloat16))
    earlier = jnp.concatenate([jnp.zeros((1, B, K), jnp.bfloat16), masked[:-1]], axis=0)
    masked_wide = masked.astype(jnp.float32)
    earlier_wide = earlier.astype(jnp.float32)
    slot_ids = jnp.arange(PAIRS, dtype=jnp.int32)
    live = (slot_ids % PAIR_DEV) < pair_count[slot_ids // PAIR_DEV]

    def right_apply(left_part, offset, right_ops):
        rolled = jnp.roll(left_part.reshape(SECTORS, B, KS, KB), -offset, axis=2)
        return jnp.einsum('sikb,kcb->sikc', rolled.astype(jnp.float32), right_ops.astype(jnp.float32))

    def one_pair(totals, pieces):
        normal_op, comp_op, rcomp_op, rnormal_op, offset, active = pieces

        def accumulate(current):
            normal_left = jnp.einsum('sij,sjk->sik', normal_op.astype(jnp.float32), masked_wide).astype(jnp.bfloat16)
            comp_left = jnp.einsum('sij,sjk->sik', comp_op.astype(jnp.float32), earlier_wide).astype(jnp.bfloat16)
            return current + right_apply(normal_left, offset, rcomp_op) + right_apply(comp_left, offset, rnormal_op)

        return lax.cond(active, accumulate, lambda current: current, totals), None

    start = jnp.zeros((SECTORS, B, KS, KB), jnp.float32)
    totals, _ = lax.scan(one_pair, start, (left_normal, left_comp, right_comp, right_normal, pair_shift, live))
    totals = totals.reshape(SECTORS, B, K)
    result = jnp.where(row_keep[:, :, None], totals, jnp.zeros((), jnp.float32))
    return result.reshape(SECTORS * B, K).astype(jnp.bfloat16)
```

```python
import jax
import jax.numpy as jnp
from jax import lax
from jax.experimental import pallas as pl
from jax.experimental.pallas import tpu as pltpu
from jax.sharding import PartitionSpec as P

B = 512
KB = 512
K = 1024
NP = 2
X_DEV = 4
ROW = 32
BF = jnp.bfloat16
F32 = jnp.float32
ANY = pl.BlockSpec(memory_space=pl.ANY)
SMEM = pl.BlockSpec(memory_space=pltpu.SMEM)
VMEM = pl.BlockSpec(memory_space=pltpu.VMEM)


def sector_call(name, terms, masked, pair_shift, pair_count, sector_rows, init=None, order=None):
    count = len(terms)
    have_init = init is not None

    def body(*refs):
        refs = list(refs)
        shift, live, rows = refs[:3]
        ins = refs[3 : 3 + 3 * count]
        pos = 3 + 3 * count
        init_ref = None
        if have_init:
            init_ref = refs[pos]
            pos += 1
        outs = refs[pos : pos + (2 if order else 1)]
        pos += len(outs)
        raw, msk, lft, rgt, acc, sems = refs[pos:]

        def src_copy(t):
            part = terms[t][1]
            return pltpu.make_async_copy(
                ins[3 * t].at[pl.ds(part * B, B), :], raw.at[t], sems.at[0, t]
            )

        def left_copy(p, t):
            return pltpu.make_async_copy(
                ins[3 * t + 1].at[p, terms[t][3]], lft.at[p, t], sems.at[1 + p, t]
            )

        def right_copy(p, t):
            return pltpu.make_async_copy(ins[3 * t + 2].at[p], rgt.at[p, t], sems.at[3 + p, t])

        def init_copy():
            return pltpu.make_async_copy(init_ref, acc, sems.at[5, 0])

        for t in range(count):
            src_copy(t).start()
            left_copy(0, t).start()
            right_copy(0, t).start()
        if have_init:
            init_copy().start()

        @pl.when(live[0] > 1)
        def _():
            for t in range(count):
                left_copy(1, t).start()
                right_copy(1, t).start()

        def work(p):
            for t in range(count):
                if p == 0:
                    src_copy(t).wait()
                    for h in range(2):
                        value = raw[t, :, h * KB : (h + 1) * KB]
                        if masked[t] is not None:
                            at = lax.broadcasted_iota(jnp.int32, (B, KB), 0)
                            value = jnp.where(at < rows[masked[t]], value, jnp.zeros((), BF))
                        msk[t, h] = value
                left_copy(p, t).wait()
                right_copy(p, t).wait()
                if have_init and p == 0 and t == 0:
                    init_copy().wait()
                for j in range(2):
                    half = (j + shift[p]) % 2
                    inner = jnp.dot(
                        lft[p, t], msk[t, half], preferred_element_type=F32
                    ).astype(BF)
                    outer = lax.dot_general(
                        inner, rgt[p, t, j], (((1,), (1,)), ((), ())), preferred_element_type=F32
                    ).reshape(16, ROW, KB)
                    if p == 0 and t == 0 and not have_init:
                        acc[j] = outer
                    else:
                        acc[j] = acc[j] + outer

        work(0)

        @pl.when(live[0] > 1)
        def _():
            work(1)

        if order is None:
            for j in range(2):
                outs[0][j] = acc[j]
        else:
            index = lax.axis_index("pairs")
            my_x = index % X_DEV
            my_z = (index // X_DEV) % 4
            for j in range(2):
                for place, rel in enumerate(order):
                    for zrel in range(4):
                        block = (my_z ^ zrel) * X_DEV + (my_x ^ rel)
                        value = acc[j, block]
                        cols = slice(j * KB, (j + 1) * KB)
                        if place < 2:
                            outs[0][place, zrel, :, cols] = value
                        else:
                            outs[1][place - 2, zrel, :, cols] = value.astype(BF)

    operands = [pair_shift, pair_count, sector_rows]
    for t in terms:
        operands += [t[0], t[2], t[4]]
    if have_init:
        operands.append(init)
    if order is None:
        out_shape = jax.ShapeDtypeStruct((2, 16, ROW, KB), F32)
        out_specs = VMEM
    else:
        out_shape = (
            jax.ShapeDtypeStruct((2, 4, ROW, K), F32),
            jax.ShapeDtypeStruct((2, 4, ROW, K), BF),
        )
        out_specs = (VMEM, VMEM)
    return pl.pallas_call(
        body,
        name=name,
        out_shape=out_shape,
        in_specs=[SMEM] * 3 + [ANY] * (len(operands) - 3),
        out_specs=out_specs,
        scratch_shapes=[
            pltpu.VMEM((count, B, K), BF),
            pltpu.VMEM((count, 2, B, KB), BF),
            pltpu.VMEM((NP, count, B, B), BF),
            pltpu.VMEM((NP, count, 2, KB, KB), BF),
            pltpu.VMEM((2, 16, ROW, KB), F32),
            pltpu.SemaphoreType.DMA((6, count)),
        ],
        compiler_params=pltpu.CompilerParams(vmem_limit_bytes=40 * 2**20),
        cost_estimate=pl.CostEstimate(
            flops=count * NP * 4 * B * B * K,
            bytes_accessed=count * 4 * 2**20 + 2 * 2**20,
            transcendentals=0,
        ),
    )(*operands)


def swap(value, mask):
    size = lax.axis_size("pairs")
    return lax.ppermute(value, "pairs", [(i, i ^ mask) for i in range(size)])


def local(
    wavefunction,
    left_normal,
    left_comp,
    right_comp,
    right_normal,
    pair_shift,
    pair_count,
    sector_rows,
):
    sects = lax.axis_size("sect")
    row_ids = jnp.arange(B, dtype=jnp.int32)
    last = jnp.where((row_ids < sector_rows[1])[:, None], wavefunction[B:], jnp.zeros((), BF))
    lower = lax.ppermute(last, "sect", [(i, i + 1) for i in range(sects - 1)])
    scal = (pair_shift, pair_count, sector_rows)

    keep_b, send_b = sector_call(
        "upper",
        [
            (wavefunction, 1, left_normal, 1, right_comp),
            (wavefunction, 0, left_comp, 1, right_normal),
        ],
        [1, 0],
        *scal,
        order=(0, 3, 1, 2),
    )
    part_a = sector_call(
        "lower_normal", [(wavefunction, 0, left_normal, 0, right_comp)], [0], *scal
    )
    keep_a, send_a = sector_call(
        "lower_comp",
        [(lower, 0, left_comp, 0, right_normal)],
        [None],
        *scal,
        init=part_a,
        order=(0, 1, 3, 2),
    )

    def x_stage(keep, send, first, second):
        got = swap(send, first)
        next_send = (keep[1] + got[1].astype(F32)).astype(BF)
        got_next = swap(next_send, second)
        return keep[0] + got[0].astype(F32) + got_next.astype(F32)

    sum_b = x_stage(keep_b, send_b, 1, 3)
    sum_a = x_stage(keep_a, send_a, 3, 1)

    index = lax.axis_index("pairs")
    high = (index // (4 * X_DEV)) % 2 == 1
    send = jnp.stack([sum_a[1], sum_a[3], sum_b[1], sum_b[3]]).astype(BF)
    got = swap(send, 1 * X_DEV).astype(F32)
    a0, a2, b0, b2 = sum_a[0] + got[0], sum_a[2] + got[1], sum_b[0] + got[2], sum_b[2] + got[3]
    own0, own2 = jnp.where(high, b0, a0), jnp.where(high, b2, a2)
    oth0, oth2 = jnp.where(high, a0, b0), jnp.where(high, a2, b2)
    got = swap(jnp.stack([own2, oth0]).astype(BF), 2 * X_DEV).astype(F32)
    own = own0 + got[0]
    got = swap((oth2 + got[1]).astype(BF), 6 * X_DEV).astype(F32)
    own = own + got
    used = jnp.where(high, sector_rows[1], sector_rows[0])
    row = (index % 16) * ROW + jnp.arange(ROW, dtype=jnp.int32)
    return jnp.where((row < used)[:, None], own, jnp.zeros((), F32)).astype(BF)


def solution(mesh):
    placed = (
        P("sect", None),
        P("pairs", "sect", None, None),
        P("pairs", "sect", None, None),
        P("pairs", None, None, None),
        P("pairs", None, None, None),
        P("pairs"),
        P("pairs"),
        P("sect"),
    )
    return jax.shard_map(
        local, mesh=mesh, in_specs=placed, out_specs=P(("sect", "pairs"), None), check_vma=False
    )
```

```python
import jax
import jax.numpy as jnp
from jax import lax
from jax.experimental import pallas as pl
from jax.experimental.pallas import tpu as pltpu
from jax.sharding import PartitionSpec as P

B = 512
KB = 512
K = 1024
NP = 2
ROW = 32
SHIFT, ROWS, LIVE = 0, 2, 4
BF = jnp.bfloat16
F32 = jnp.float32
ANY = pl.BlockSpec(memory_space=pl.ANY)
HBM = pl.BlockSpec(memory_space=pltpu.HBM)
SMEM = pl.BlockSpec(memory_space=pltpu.SMEM)
VMEM = pl.BlockSpec(memory_space=pltpu.VMEM)


NT = (((1,), (1,)), ((), ()))


def masked_rows(value, first_row, used):
    at = lax.broadcasted_iota(jnp.int32, value.shape, 0) + first_row
    return jnp.where(at < used, value, jnp.zeros((), BF))


def for_live(live, act):
    for pairs in range(1, NP + 1):

        @pl.when(live == pairs)
        def _():
            act(pairs)


def left_product(left, source, inner, shift, pairs, terms, term):
    out = jnp.dot(left, source[...], preferred_element_type=F32).astype(BF)
    rows = out.shape[0] // pairs
    for p in range(pairs):
        for half in range(2):
            at = (p * terms + term) * KB
            inner[(half + shift[p]) & 1, :, at : at + KB] = out[
                p * rows : (p + 1) * rows, half * KB : (half + 1) * KB
            ]


def row_groups(places):
    index = lax.axis_index("pairs")
    my_x, parity = index & 3, (index >> 2) & 1
    first, second = pair_order(lax.axis_index("sect"))
    rels = (0, second, first, 2)
    return [
        (2 * (zplace % 2) + (parity ^ (zplace // 2))) * 4 + (my_x ^ rels[place])
        for place in places
        for zplace in range(4)
    ]


def cost(flops, mib):
    return pl.CostEstimate(flops=flops, bytes_accessed=mib * 2**20, transcendentals=0)


def limit(mib):
    return pltpu.CompilerParams(vmem_limit_bytes=mib * 2**20)


def mask_last(sector_rows, wavefunction):
    chunk = B // 4

    def body(rows_ref, wave, out, buf, rows, sems):
        copies = [
            pltpu.make_async_copy(
                wave.at[pl.ds(B + c * chunk, chunk), :], buf.at[pl.ds(c * chunk, chunk), :], sems.at[c]
            )
            for c in range(4)
        ]
        count = pltpu.make_async_copy(rows_ref, rows, sems.at[4])
        count.start()
        for copy in copies:
            copy.start()
        count.wait()
        for c, copy in enumerate(copies):
            copy.wait()
            part = slice(c * chunk, (c + 1) * chunk)
            out[part, :] = masked_rows(buf[part, :], c * chunk, rows[1])

    return pl.pallas_call(
        body,
        name="mask_last",
        out_shape=jax.ShapeDtypeStruct((B, K), BF),
        in_specs=[HBM] * 2,
        out_specs=VMEM,
        scratch_shapes=[
            pltpu.VMEM((B, K), BF),
            pltpu.SMEM((2,), jnp.int32),
            pltpu.SemaphoreType.DMA((5,)),
        ],
        compiler_params=limit(8),
        cost_estimate=cost(B * K, 2),
    )(sector_rows, wavefunction)


def upper_call(pair_count, pair_shift, sector_rows, mask_b, wavefunction, left_normal, left_comp, right_comp, right_normal):
    def body(
        cnt, shift_ref, rows_ref, m_b, wave, ln, lc, rc, rn,
        keep, send, scal, m_a, l_na, l_ca, right,
        raw, l_nb, l_cb, inner, acc, shift, rows, sems,
    ):
        wave_copy = pltpu.make_async_copy(wave.at[pl.ds(0, B), :], raw, sems.at[0])

        def left_copies(source, sector, target, size, sem):
            return [
                pltpu.make_async_copy(
                    source.at[p, sector], target.at[pl.ds(p * size, size)], sems.at[sem + p]
                )
                for p in range(NP)
            ]

        def right_copies(source, term, sem):
            return [
                pltpu.make_async_copy(
                    source.at[p], right.at[:, :, pl.ds((p * 2 + term) * KB, KB)], sems.at[sem + p]
                )
                for p in range(NP)
            ]

        normal_b = left_copies(ln, 1, l_nb, B, 1)
        comp_b = left_copies(lc, 1, l_cb, 16, 3)
        rights = right_copies(rc, 0, 5) + right_copies(rn, 1, 7)
        lower = left_copies(ln, 0, l_na, B, 9) + left_copies(lc, 0, l_ca, 16, 11)
        scalars = [
            pltpu.make_async_copy(shift_ref, shift, sems.at[13]),
            pltpu.make_async_copy(rows_ref, rows, sems.at[14]),
        ]
        for copy in scalars + normal_b + [wave_copy] + comp_b + rights:
            copy.start()
        for copy in scalars:
            copy.wait()
        for i in range(2):
            scal[SHIFT + i] = shift[i]
            scal[ROWS + i] = rows[i]
        scal[LIVE] = cnt[0]
        for copy in normal_b:
            copy.wait()
        for_live(
            cnt[0], lambda pairs: left_product(l_nb[: pairs * B, :], m_b, inner, shift, pairs, 2, 0)
        )
        for copy in lower:
            copy.start()
        wave_copy.wait()
        m_a[...] = masked_rows(raw[...], 0, rows[0])
        for copy in comp_b:
            copy.wait()
        for_live(
            cnt[0],
            lambda pairs: left_product(
                l_cb[: pairs * 16].reshape(pairs * B, B), m_a, inner, shift, pairs, 2, 1
            ),
        )
        for copy in rights:
            copy.wait()

        def finish(pairs):
            for j in range(2):
                acc[j] = lax.dot_general(
                    inner[j, :, : 2 * pairs * KB],
                    right[j, :, : 2 * pairs * KB],
                    NT,
                    preferred_element_type=F32,
                ).reshape(16, ROW, KB)

        for_live(cnt[0], finish)
        for i, group in enumerate(row_groups(range(4))):
            for j in range(2):
                cols = slice(j * KB, (j + 1) * KB)
                value = acc[j, group]
                if i < 8:
                    keep[i // 4, i % 4, :, cols] = value
                else:
                    send[i // 4 - 2, i % 4, :, cols] = value.astype(BF)
        for copy in lower:
            copy.wait()

    return pl.pallas_call(
        body,
        name="upper",
        out_shape=(
            jax.ShapeDtypeStruct((2, 4, ROW, K), F32),
            jax.ShapeDtypeStruct((2, 4, ROW, K), BF),
            jax.ShapeDtypeStruct((8,), jnp.int32),
            jax.ShapeDtypeStruct((B, K), BF),
            jax.ShapeDtypeStruct((NP * B, B), BF),
            jax.ShapeDtypeStruct((NP * 16, ROW, B), BF),
            jax.ShapeDtypeStruct((2, KB, 2 * NP * KB), BF),
        ),
        in_specs=[SMEM, HBM, HBM, VMEM] + [HBM] * 5,
        out_specs=(VMEM, VMEM, SMEM) + (VMEM,) * 4,
        scratch_shapes=[
            pltpu.VMEM((B, K), BF),
            pltpu.VMEM((NP * B, B), BF),
            pltpu.VMEM((NP * 16, ROW, B), BF),
            pltpu.VMEM((2, B, 2 * NP * KB), BF),
            pltpu.VMEM((2, 16, ROW, KB), F32),
            pltpu.SMEM((2,), jnp.int32),
            pltpu.SMEM((2,), jnp.int32),
            pltpu.SemaphoreType.DMA((15,)),
        ],
        compiler_params=limit(28),
        cost_estimate=cost(2 * NP * 4 * B * B * K, 10),
    )(
        pair_count,
        pair_shift,
        sector_rows,
        mask_b,
        wavefunction,
        left_normal,
        left_comp,
        right_comp,
        right_normal,
    )


def right_product(inner, right, j, term, pairs):
    ops = [right[j, :, (p * 2 + term) * KB : (p * 2 + term + 1) * KB] for p in range(pairs)]
    return lax.dot_general(
        inner[j, :, : pairs * KB],
        jnp.concatenate(ops, axis=1) if pairs > 1 else ops[0],
        NT,
        preferred_element_type=F32,
    )


def lower_normal(scalars, source, left, right):
    def body(scal, src, lft, rgt, out, inner):
        def act(pairs):
            left_product(lft[: pairs * B, :], src, inner, scal, pairs, 1, 0)
            for j in range(2):
                out[j] = right_product(inner, rgt, j, 0, pairs).reshape(16, ROW, KB)

        for_live(scal[LIVE], act)

    return pl.pallas_call(
        body,
        name="lower_normal",
        out_shape=jax.ShapeDtypeStruct((2, 16, ROW, KB), F32),
        in_specs=[SMEM] + [VMEM] * 3,
        out_specs=VMEM,
        scratch_shapes=[pltpu.VMEM((2, B, NP * KB), BF)],
        compiler_params=limit(20),
        cost_estimate=cost(NP * 4 * B * B * K, 4),
    )(scalars, source, left, right)


def lower_comp(name, places, dtype, scalars, source, left, right, partial):
    def body(scal, src, lft, rgt, part, out, inner):
        groups = row_groups(places)

        def act(pairs):
            rows = [lft[p * 16 + group] for p in range(pairs) for group in groups]
            left_product(jnp.concatenate(rows, axis=0), src, inner, scal, pairs, 1, 0)
            for j in range(2):
                cols = slice(j * KB, (j + 1) * KB)
                total = right_product(inner, rgt, j, 1, pairs).reshape(8, ROW, KB)
                for i, group in enumerate(groups):
                    out[i // 4, i % 4, :, cols] = (part[j, group] + total[i]).astype(dtype)

        for_live(scal[LIVE], act)

    return pl.pallas_call(
        body,
        name=name,
        out_shape=jax.ShapeDtypeStruct((2, 4, ROW, K), dtype),
        in_specs=[SMEM] + [VMEM] * 4,
        out_specs=VMEM,
        scratch_shapes=[pltpu.VMEM((2, B // 2, NP * KB), BF)],
        compiler_params=limit(20),
        cost_estimate=cost(NP * 2 * B * B * K, 4),
    )(scalars, source, left, right, partial)


def pair_order(sect):
    core = sect & 1
    return 1 + 2 * core, 3 - 2 * core


def x_partner(step):
    return lambda x, z, sect: (x ^ pair_order(sect)[step], z)


def z_neighbour(x, z, sect):
    return (x, z ^ 1) if sect & 1 == 0 else (x, (z + 1 if z & 1 else z - 1) % 8)


def z_partner(step):
    return lambda x, z, sect: (x, z ^ (2 * pair_order(sect)[step]))


def swap(value, partner):
    sects = lax.axis_size("sect")
    moves = []
    for index in range(lax.axis_size("pairs")):
        for sect in range(sects):
            x, z = partner(index & 3, index >> 2, sect)
            moves.append((index * sects + sect, (z * 4 + x) * sects + sect))
    return lax.ppermute(value, ("pairs", "sect"), moves)


def local(
    wavefunction,
    left_normal,
    left_comp,
    right_comp,
    right_normal,
    pair_shift,
    pair_count,
    sector_rows,
):
    sects = lax.axis_size("sect")
    (
        wavefunction,
        left_normal,
        left_comp,
        right_comp,
        right_normal,
        pair_shift,
        sector_rows,
    ) = (
        pltpu.with_memory_space_constraint(value, pltpu.HBM)
        for value in (
            wavefunction,
            left_normal,
            left_comp.reshape(NP, 2, 16, ROW, B),
            right_comp,
            right_normal,
            pair_shift,
            sector_rows,
        )
    )
    last = mask_last(sector_rows, wavefunction)
    lower = lax.ppermute(last, "sect", [(i, i + 1) for i in range(sects - 1)])
    keep_b, send_b, scalars, mask_a, left_na, left_ca, right = upper_call(
        pair_count,
        pair_shift,
        sector_rows,
        last,
        wavefunction,
        left_normal,
        left_comp,
        right_comp,
        right_normal,
    )
    part_a = lower_normal(scalars, mask_a, left_na, right)
    comp = (scalars, lower, left_ca, right, part_a)
    send_a = lower_comp("lower_send", (2, 3), BF, *comp)
    keep_a = lower_comp("lower_keep", (0, 1), F32, *comp)

    got_b = swap(send_b, x_partner(0))
    got_a = swap(send_a, x_partner(0))
    got_a, got_b = lax.optimization_barrier((got_a, got_b))
    sum_a = keep_a + got_a.astype(F32)
    send_a = sum_a[1].astype(BF)
    sum_b = keep_b + got_b.astype(F32)
    got_a = swap(send_a, x_partner(1))
    got_b = swap(sum_b[:, 2:].astype(BF), z_neighbour)
    got_a, got_b = lax.optimization_barrier((got_a, got_b))
    sum_a = sum_a[0] + got_a.astype(F32)
    send_a = sum_a[2:].astype(BF)
    sum_b = sum_b[:, :2] + got_b.astype(F32)
    got_a = swap(send_a, z_neighbour)
    got_b = swap(sum_b[1].astype(BF), x_partner(1))
    kept = jnp.concatenate([sum_a[:2] + got_a.astype(F32), sum_b[0] + got_b.astype(F32)])

    index = lax.axis_index("pairs")
    group = index >> 3
    first, second = pair_order(lax.axis_index("sect"))

    def pick(value, at):
        return lax.dynamic_index_in_dim(value, at, 0, keepdims=False)

    send = jnp.stack([pick(kept, group ^ first), pick(kept, group ^ 2)]).astype(BF)
    got = swap(send, z_partner(0))
    got_last = swap((pick(kept, group ^ second) + got[1].astype(F32)).astype(BF), z_partner(1))
    own = pick(kept, group) + got[0].astype(F32) + got_last.astype(F32)
    used = lax.dynamic_index_in_dim(scalars, ROWS + (group >> 1), 0)
    row = (index & 15) * ROW + lax.broadcasted_iota(jnp.int32, (ROW, K), 0)
    return jnp.where(row < used[None, :], own, jnp.zeros((), F32)).astype(BF)


def solution(mesh):
    placed = (
        P("sect", None),
        P("pairs", "sect", None, None),
        P("pairs", "sect", None, None),
        P("pairs", None, None, None),
        P("pairs", None, None, None),
        P("pairs"),
        P("pairs"),
        P("sect"),
    )
    return jax.shard_map(
        local, mesh=mesh, in_specs=placed, out_specs=P(("sect", "pairs"), None), check_vma=False
    )
```

```python
import jax
import jax.numpy as jnp
from jax import lax
from jax.experimental import pallas as pl
from jax.experimental.pallas import tpu as pltpu
from jax.sharding import PartitionSpec as P

B = 512
KB = 512
K = 1024
NP = 2
ROW = 32
SHIFT, ROWS, LIVE = 0, 2, 4
BF = jnp.bfloat16
F32 = jnp.float32
ANY = pl.BlockSpec(memory_space=pl.ANY)
HBM = pl.BlockSpec(memory_space=pltpu.HBM)
SMEM = pl.BlockSpec(memory_space=pltpu.SMEM)
VMEM = pl.BlockSpec(memory_space=pltpu.VMEM)


NT = (((1,), (1,)), ((), ()))


def masked_rows(value, first_row, used):
    at = lax.broadcasted_iota(jnp.int32, value.shape, 0) + first_row
    return jnp.where(at < used, value, jnp.zeros((), BF))


def for_live(live, act):
    for pairs in range(1, NP + 1):

        @pl.when(live == pairs)
        def _():
            act(pairs)


def left_product(left, source, inner, shift, pairs, terms, term):
    out = jnp.dot(left, source[...], preferred_element_type=F32).astype(BF)
    rows = out.shape[0] // pairs
    for p in range(pairs):
        for half in range(2):
            at = (p * terms + term) * KB
            inner[(half + shift[p]) & 1, :, at : at + KB] = out[
                p * rows : (p + 1) * rows, half * KB : (half + 1) * KB
            ]


def row_groups(places):
    index = lax.axis_index("pairs")
    my_x, parity = index & 3, (index >> 2) & 1
    first, second = pair_order(lax.axis_index("sect"))
    rels = (0, second, first, 2)
    return [
        (2 * (zplace % 2) + (parity ^ (zplace // 2))) * 4 + (my_x ^ rels[place])
        for place in places
        for zplace in range(4)
    ]


def cost(flops, mib):
    return pl.CostEstimate(flops=flops, bytes_accessed=mib * 2**20, transcendentals=0)


def limit(mib):
    return pltpu.CompilerParams(vmem_limit_bytes=mib * 2**20)


def mask_last(sector_rows, wavefunction):
    chunk = B // 4

    def body(rows_ref, wave, out, buf, rows, sems):
        copies = [
            pltpu.make_async_copy(
                wave.at[pl.ds(B + c * chunk, chunk), :], buf.at[pl.ds(c * chunk, chunk), :], sems.at[c]
            )
            for c in range(4)
        ]
        count = pltpu.make_async_copy(rows_ref, rows, sems.at[4])
        count.start()
        for copy in copies:
            copy.start()
        count.wait()
        for c, copy in enumerate(copies):
            copy.wait()
            part = slice(c * chunk, (c + 1) * chunk)
            out[part, :] = masked_rows(buf[part, :], c * chunk, rows[1])

    return pl.pallas_call(
        body,
        name="mask_last",
        out_shape=jax.ShapeDtypeStruct((B, K), BF),
        in_specs=[HBM] * 2,
        out_specs=VMEM,
        scratch_shapes=[
            pltpu.VMEM((B, K), BF),
            pltpu.SMEM((2,), jnp.int32),
            pltpu.SemaphoreType.DMA((5,)),
        ],
        compiler_params=limit(8),
        cost_estimate=cost(B * K, 2),
    )(sector_rows, wavefunction)


def upper_call(pair_count, pair_shift, sector_rows, mask_b, wavefunction, left_normal, left_comp, right_comp, right_normal):
    def body(
        cnt, shift_ref, rows_ref, m_b, wave, ln, lc, rc, rn,
        keep, send, scal, m_a, l_na, l_ca, right,
        raw, l_nb, l_cb, inner, acc, shift, rows, sems,
    ):
        wave_copy = pltpu.make_async_copy(wave.at[pl.ds(0, B), :], raw, sems.at[0])

        def left_copies(source, sector, target, size, sem):
            return [
                pltpu.make_async_copy(
                    source.at[p, sector], target.at[pl.ds(p * size, size)], sems.at[sem + p]
                )
                for p in range(NP)
            ]

        def right_copies(source, term, sem):
            return [
                pltpu.make_async_copy(
                    source.at[p], right.at[:, :, pl.ds((p * 2 + term) * KB, KB)], sems.at[sem + p]
                )
                for p in range(NP)
            ]

        normal_b = left_copies(ln, 1, l_nb, B, 1)
        comp_b = left_copies(lc, 1, l_cb, 16, 3)
        rights = right_copies(rc, 0, 5) + right_copies(rn, 1, 7)
        lower = left_copies(ln, 0, l_na, B, 9) + left_copies(lc, 0, l_ca, 16, 11)
        scalars = [
            pltpu.make_async_copy(shift_ref, shift, sems.at[13]),
            pltpu.make_async_copy(rows_ref, rows, sems.at[14]),
        ]
        for copy in scalars + normal_b + [wave_copy] + comp_b + rights:
            copy.start()
        for copy in scalars:
            copy.wait()
        for i in range(2):
            scal[SHIFT + i] = shift[i]
            scal[ROWS + i] = rows[i]
        scal[LIVE] = cnt[0]
        for copy in normal_b:
            copy.wait()
        for_live(
            cnt[0], lambda pairs: left_product(l_nb[: pairs * B, :], m_b, inner, shift, pairs, 2, 0)
        )
        for copy in lower:
            copy.start()
        wave_copy.wait()
        m_a[...] = masked_rows(raw[...], 0, rows[0])
        for copy in comp_b:
            copy.wait()
        for_live(
            cnt[0],
            lambda pairs: left_product(
                l_cb[: pairs * 16].reshape(pairs * B, B), m_a, inner, shift, pairs, 2, 1
            ),
        )
        for copy in rights:
            copy.wait()

        def finish(pairs):
            for j in range(2):
                acc[j] = lax.dot_general(
                    inner[j, :, : 2 * pairs * KB],
                    right[j, :, : 2 * pairs * KB],
                    NT,
                    preferred_element_type=F32,
                ).reshape(16, ROW, KB)

        for_live(cnt[0], finish)
        for i, group in enumerate(row_groups(range(4))):
            for j in range(2):
                cols = slice(j * KB, (j + 1) * KB)
                value = acc[j, group]
                if i < 8:
                    keep[i // 4, i % 4, :, cols] = value
                else:
                    send[i // 4 - 2, i % 4, :, cols] = value.astype(BF)
        for copy in lower:
            copy.wait()

    return pl.pallas_call(
        body,
        name="upper",
        out_shape=(
            jax.ShapeDtypeStruct((2, 4, ROW, K), F32),
            jax.ShapeDtypeStruct((2, 4, ROW, K), BF),
            jax.ShapeDtypeStruct((8,), jnp.int32),
            jax.ShapeDtypeStruct((B, K), BF),
            jax.ShapeDtypeStruct((NP * B, B), BF),
            jax.ShapeDtypeStruct((NP * 16, ROW, B), BF),
            jax.ShapeDtypeStruct((2, KB, 2 * NP * KB), BF),
        ),
        in_specs=[SMEM, HBM, HBM, VMEM] + [HBM] * 5,
        out_specs=(VMEM, VMEM, SMEM) + (VMEM,) * 4,
        scratch_shapes=[
            pltpu.VMEM((B, K), BF),
            pltpu.VMEM((NP * B, B), BF),
            pltpu.VMEM((NP * 16, ROW, B), BF),
            pltpu.VMEM((2, B, 2 * NP * KB), BF),
            pltpu.VMEM((2, 16, ROW, KB), F32),
            pltpu.SMEM((2,), jnp.int32),
            pltpu.SMEM((2,), jnp.int32),
            pltpu.SemaphoreType.DMA((15,)),
        ],
        compiler_params=limit(20),
        cost_estimate=cost(2 * NP * 4 * B * B * K, 10),
    )(
        pair_count,
        pair_shift,
        sector_rows,
        mask_b,
        wavefunction,
        left_normal,
        left_comp,
        right_comp,
        right_normal,
    )


def right_product(inner, right, j, term, pairs):
    ops = [right[j, :, (p * 2 + term) * KB : (p * 2 + term + 1) * KB] for p in range(pairs)]
    return lax.dot_general(
        inner[j, :, : pairs * KB],
        jnp.concatenate(ops, axis=1) if pairs > 1 else ops[0],
        NT,
        preferred_element_type=F32,
    )


def lower_normal(scalars, source, left, right):
    def body(scal, src, lft, rgt, out, inner):
        def act(pairs):
            left_product(lft[: pairs * B, :], src, inner, scal, pairs, 1, 0)
            for j in range(2):
                out[j] = right_product(inner, rgt, j, 0, pairs).reshape(16, ROW, KB)

        for_live(scal[LIVE], act)

    return pl.pallas_call(
        body,
        name="lower_normal",
        out_shape=jax.ShapeDtypeStruct((2, 16, ROW, KB), F32),
        in_specs=[SMEM] + [VMEM] * 3,
        out_specs=VMEM,
        scratch_shapes=[pltpu.VMEM((2, B, NP * KB), BF)],
        compiler_params=limit(20),
        cost_estimate=cost(NP * 4 * B * B * K, 4),
    )(scalars, source, left, right)


def lower_comp(name, places, dtype, scalars, source, left, right, partial):
    def body(scal, src, lft, rgt, part, out, inner):
        groups = row_groups(places)

        def act(pairs):
            rows = [lft[p * 16 + group] for p in range(pairs) for group in groups]
            left_product(jnp.concatenate(rows, axis=0), src, inner, scal, pairs, 1, 0)
            for j in range(2):
                cols = slice(j * KB, (j + 1) * KB)
                total = right_product(inner, rgt, j, 1, pairs).reshape(8, ROW, KB)
                for i, group in enumerate(groups):
                    out[i // 4, i % 4, :, cols] = (part[j, group] + total[i]).astype(dtype)

        for_live(scal[LIVE], act)

    return pl.pallas_call(
        body,
        name=name,
        out_shape=jax.ShapeDtypeStruct((2, 4, ROW, K), dtype),
        in_specs=[SMEM] + [VMEM] * 4,
        out_specs=VMEM,
        scratch_shapes=[pltpu.VMEM((2, B // 2, NP * KB), BF)],
        compiler_params=limit(20),
        cost_estimate=cost(NP * 2 * B * B * K, 4),
    )(scalars, source, left, right, partial)


def pair_order(sect):
    core = sect & 1
    return 1 + 2 * core, 3 - 2 * core


def x_partner(step):
    return lambda x, z, sect: (x ^ pair_order(sect)[step], z)


def z_neighbour(x, z, sect):
    return (x, z ^ 1) if sect & 1 == 0 else (x, (z + 1 if z & 1 else z - 1) % 8)


def z_group(mask):
    return lambda x, z, sect: (x, z ^ (2 * mask))


def swap(value, partner):
    sects = lax.axis_size("sect")
    moves = []
    for index in range(lax.axis_size("pairs")):
        for sect in range(sects):
            x, z = partner(index & 3, index >> 2, sect)
            moves.append((index * sects + sect, (z * 4 + x) * sects + sect))
    return lax.ppermute(value, ("pairs", "sect"), moves)


def local(
    wavefunction,
    left_normal,
    left_comp,
    right_comp,
    right_normal,
    pair_shift,
    pair_count,
    sector_rows,
):
    sects = lax.axis_size("sect")
    (
        wavefunction,
        left_normal,
        left_comp,
        right_comp,
        right_normal,
        pair_shift,
        sector_rows,
    ) = (
        pltpu.with_memory_space_constraint(value, pltpu.HBM)
        for value in (
            wavefunction,
            left_normal,
            left_comp.reshape(NP, 2, 16, ROW, B),
            right_comp,
            right_normal,
            pair_shift,
            sector_rows,
        )
    )
    last = mask_last(sector_rows, wavefunction)
    lower = lax.ppermute(last, "sect", [(i, i + 1) for i in range(sects - 1)])
    keep_b, send_b, scalars, mask_a, left_na, left_ca, right = upper_call(
        pair_count,
        pair_shift,
        sector_rows,
        last,
        wavefunction,
        left_normal,
        left_comp,
        right_comp,
        right_normal,
    )
    part_a = lower_normal(scalars, mask_a, left_na, right)
    comp = (scalars, lower, left_ca, right, part_a)
    send_a = lower_comp("lower_send", (2, 3), BF, *comp)
    keep_a = lower_comp("lower_keep", (0, 1), F32, *comp)

    got_b = swap(send_b, x_partner(0))
    got_a = swap(send_a, x_partner(0))
    got_b, keep_a = lax.optimization_barrier((got_b, keep_a))
    sum_b = keep_b + got_b.astype(F32)
    got_b = swap(sum_b[:, 2:].astype(BF), z_neighbour)
    sum_a = keep_a + got_a.astype(F32)
    send_a = sum_a[1].astype(BF)
    send_a, got_b = lax.optimization_barrier((send_a, got_b))
    sum_b = sum_b[:, :2] + got_b.astype(F32)
    got = swap(jnp.concatenate([send_a, sum_b[1].astype(BF)]), x_partner(1))
    got_a, got_b = got[:4], got[4:]
    sum_a = sum_a[0] + got_a.astype(F32)
    got_a = swap(sum_a[2:].astype(BF), z_neighbour)
    kept = jnp.concatenate([sum_a[:2] + got_a.astype(F32), sum_b[0] + got_b.astype(F32)])

    index = lax.axis_index("pairs")
    group = index >> 3

    def pick(value, at):
        return lax.dynamic_index_in_dim(value, at, 0, keepdims=False)

    own = pick(kept, group)
    for mask in (2, 3, 1):
        got = swap(pick(kept, group ^ mask).astype(BF), z_group(mask))
        own = own + got.astype(F32)
    used = lax.dynamic_index_in_dim(scalars, ROWS + (group >> 1), 0)
    row = (index & 15) * ROW + lax.broadcasted_iota(jnp.int32, (ROW, K), 0)
    return jnp.where(row < used[None, :], own, jnp.zeros((), F32)).astype(BF)


def solution(mesh):
    placed = (
        P("sect", None),
        P("pairs", "sect", None, None),
        P("pairs", "sect", None, None),
        P("pairs", None, None, None),
        P("pairs", None, None, None),
        P("pairs"),
        P("pairs"),
        P("sect"),
    )
    return jax.shard_map(
        local, mesh=mesh, in_specs=placed, out_specs=P(("sect", "pairs"), None), check_vma=False
    )
```

```python
import jax
import jax.numpy as jnp
from jax import lax
from jax.experimental import pallas as pl
from jax.experimental.pallas import tpu as pltpu
from jax.sharding import PartitionSpec as P

B = 512
KB = 512
K = 1024
NP = 2
ROW = 32
SHIFT, ROWS, LIVE = 0, 2, 4
BF = jnp.bfloat16
F32 = jnp.float32
ANY = pl.BlockSpec(memory_space=pl.ANY)
HBM = pl.BlockSpec(memory_space=pltpu.HBM)
SMEM = pl.BlockSpec(memory_space=pltpu.SMEM)
VMEM = pl.BlockSpec(memory_space=pltpu.VMEM)


NT = (((1,), (1,)), ((), ()))


def masked_rows(value, first_row, used):
    at = lax.broadcasted_iota(jnp.int32, value.shape, 0) + first_row
    return jnp.where(at < used, value, jnp.zeros((), BF))


def for_live(live, act):
    for pairs in range(1, NP + 1):

        @pl.when(live == pairs)
        def _():
            act(pairs)


def left_product(left, source, inner, shift, pairs, terms, term):
    out = jnp.dot(left, source[...], preferred_element_type=F32).astype(BF)
    rows = out.shape[0] // pairs
    for p in range(pairs):
        for half in range(2):
            at = (p * terms + term) * KB
            inner[(half + shift[p]) & 1, :, at : at + KB] = out[
                p * rows : (p + 1) * rows, half * KB : (half + 1) * KB
            ]


def row_groups(places):
    index = lax.axis_index("pairs")
    my_x, parity = index & 3, (index >> 2) & 1
    first, second = pair_order(lax.axis_index("sect"))
    rels = (0, second, first, 2)
    return [
        (2 * (zplace % 2) + (parity ^ (zplace // 2))) * 4 + (my_x ^ rels[place])
        for place in places
        for zplace in range(4)
    ]


def cost(flops, mib):
    return pl.CostEstimate(flops=flops, bytes_accessed=mib * 2**20, transcendentals=0)


def limit(mib):
    return pltpu.CompilerParams(vmem_limit_bytes=mib * 2**20)


def mask_last(sector_rows, wavefunction):
    chunk = B // 4

    def body(rows_ref, wave, out, buf, rows, sems):
        copies = [
            pltpu.make_async_copy(
                wave.at[pl.ds(B + c * chunk, chunk), :], buf.at[pl.ds(c * chunk, chunk), :], sems.at[c]
            )
            for c in range(4)
        ]
        count = pltpu.make_async_copy(rows_ref, rows, sems.at[4])
        count.start()
        for copy in copies:
            copy.start()
        count.wait()
        for c, copy in enumerate(copies):
            copy.wait()
            part = slice(c * chunk, (c + 1) * chunk)
            out[part, :] = masked_rows(buf[part, :], c * chunk, rows[1])

    return pl.pallas_call(
        body,
        name="mask_last",
        out_shape=jax.ShapeDtypeStruct((B, K), BF),
        in_specs=[HBM] * 2,
        out_specs=VMEM,
        scratch_shapes=[
            pltpu.VMEM((B, K), BF),
            pltpu.SMEM((2,), jnp.int32),
            pltpu.SemaphoreType.DMA((5,)),
        ],
        compiler_params=limit(8),
        cost_estimate=cost(B * K, 2),
    )(sector_rows, wavefunction)


def upper_call(pair_count, pair_shift, sector_rows, mask_b, wavefunction, left_normal, left_comp, right_comp, right_normal):
    def body(
        cnt, shift_ref, rows_ref, m_b, wave, ln, lc, rc, rn,
        keep, send, scal, m_a, l_na, l_ca, right,
        raw, l_nb, l_cb, inner, acc, shift, rows, sems,
    ):
        wave_copy = pltpu.make_async_copy(wave.at[pl.ds(0, B), :], raw, sems.at[0])

        def left_copies(source, sector, target, size, sem):
            return [
                pltpu.make_async_copy(
                    source.at[p, sector], target.at[pl.ds(p * size, size)], sems.at[sem + p]
                )
                for p in range(NP)
            ]

        def right_copies(source, term, sem):
            return [
                pltpu.make_async_copy(
                    source.at[p], right.at[:, :, pl.ds((p * 2 + term) * KB, KB)], sems.at[sem + p]
                )
                for p in range(NP)
            ]

        normal_b = left_copies(ln, 1, l_nb, B, 1)
        comp_b = left_copies(lc, 1, l_cb, 16, 3)
        rights = right_copies(rc, 0, 5) + right_copies(rn, 1, 7)
        lower = left_copies(ln, 0, l_na, B, 9) + left_copies(lc, 0, l_ca, 16, 11)
        scalars = [
            pltpu.make_async_copy(shift_ref, shift, sems.at[13]),
            pltpu.make_async_copy(rows_ref, rows, sems.at[14]),
        ]
        for copy in scalars + normal_b + [wave_copy] + comp_b + rights:
            copy.start()
        for copy in scalars:
            copy.wait()
        for i in range(2):
            scal[SHIFT + i] = shift[i]
            scal[ROWS + i] = rows[i]
        scal[LIVE] = cnt[0]
        for copy in normal_b:
            copy.wait()
        for_live(
            cnt[0], lambda pairs: left_product(l_nb[: pairs * B, :], m_b, inner, shift, pairs, 2, 0)
        )
        for copy in lower:
            copy.start()
        wave_copy.wait()
        m_a[...] = masked_rows(raw[...], 0, rows[0])
        for copy in comp_b:
            copy.wait()
        for_live(
            cnt[0],
            lambda pairs: left_product(
                l_cb[: pairs * 16].reshape(pairs * B, B), m_a, inner, shift, pairs, 2, 1
            ),
        )
        for copy in rights:
            copy.wait()

        def finish(pairs):
            for j in range(2):
                acc[j] = lax.dot_general(
                    inner[j, :, : 2 * pairs * KB],
                    right[j, :, : 2 * pairs * KB],
                    NT,
                    preferred_element_type=F32,
                ).reshape(16, ROW, KB)

        for_live(cnt[0], finish)
        for i, group in enumerate(row_groups(range(4))):
            for j in range(2):
                cols = slice(j * KB, (j + 1) * KB)
                value = acc[j, group]
                if i < 8:
                    keep[i // 4, i % 4, :, cols] = value
                else:
                    send[i // 4 - 2, i % 4, :, cols] = value.astype(BF)
        for copy in lower:
            copy.wait()

    return pl.pallas_call(
        body,
        name="upper",
        out_shape=(
            jax.ShapeDtypeStruct((2, 4, ROW, K), F32),
            jax.ShapeDtypeStruct((2, 4, ROW, K), BF),
            jax.ShapeDtypeStruct((8,), jnp.int32),
            jax.ShapeDtypeStruct((B, K), BF),
            jax.ShapeDtypeStruct((NP * B, B), BF),
            jax.ShapeDtypeStruct((NP * 16, ROW, B), BF),
            jax.ShapeDtypeStruct((2, KB, 2 * NP * KB), BF),
        ),
        in_specs=[SMEM, HBM, HBM, VMEM] + [HBM] * 5,
        out_specs=(VMEM, VMEM, SMEM) + (VMEM,) * 4,
        scratch_shapes=[
            pltpu.VMEM((B, K), BF),
            pltpu.VMEM((NP * B, B), BF),
            pltpu.VMEM((NP * 16, ROW, B), BF),
            pltpu.VMEM((2, B, 2 * NP * KB), BF),
            pltpu.VMEM((2, 16, ROW, KB), F32),
            pltpu.SMEM((2,), jnp.int32),
            pltpu.SMEM((2,), jnp.int32),
            pltpu.SemaphoreType.DMA((15,)),
        ],
        compiler_params=limit(20),
        cost_estimate=cost(2 * NP * 4 * B * B * K, 10),
    )(
        pair_count,
        pair_shift,
        sector_rows,
        mask_b,
        wavefunction,
        left_normal,
        left_comp,
        right_comp,
        right_normal,
    )


def right_product(inner, right, j, term, pairs):
    ops = [right[j, :, (p * 2 + term) * KB : (p * 2 + term + 1) * KB] for p in range(pairs)]
    return lax.dot_general(
        inner[j, :, : pairs * KB],
        jnp.concatenate(ops, axis=1) if pairs > 1 else ops[0],
        NT,
        preferred_element_type=F32,
    )


def lower_normal(scalars, source, left, right):
    def body(scal, src, lft, rgt, out, inner):
        def act(pairs):
            left_product(lft[: pairs * B, :], src, inner, scal, pairs, 1, 0)
            for j in range(2):
                out[j] = right_product(inner, rgt, j, 0, pairs).reshape(16, ROW, KB)

        for_live(scal[LIVE], act)

    return pl.pallas_call(
        body,
        name="lower_normal",
        out_shape=jax.ShapeDtypeStruct((2, 16, ROW, KB), F32),
        in_specs=[SMEM] + [VMEM] * 3,
        out_specs=VMEM,
        scratch_shapes=[pltpu.VMEM((2, B, NP * KB), BF)],
        compiler_params=limit(20),
        cost_estimate=cost(NP * 4 * B * B * K, 4),
    )(scalars, source, left, right)


def lower_comp(name, places, dtype, scalars, source, left, right, partial):
    def body(scal, src, lft, rgt, part, out, inner):
        groups = row_groups(places)

        def act(pairs):
            rows = [lft[p * 16 + group] for p in range(pairs) for group in groups]
            left_product(jnp.concatenate(rows, axis=0), src, inner, scal, pairs, 1, 0)
            for j in range(2):
                cols = slice(j * KB, (j + 1) * KB)
                total = right_product(inner, rgt, j, 1, pairs).reshape(8, ROW, KB)
                for i, group in enumerate(groups):
                    out[i // 4, i % 4, :, cols] = (part[j, group] + total[i]).astype(dtype)

        for_live(scal[LIVE], act)

    return pl.pallas_call(
        body,
        name=name,
        out_shape=jax.ShapeDtypeStruct((2, 4, ROW, K), dtype),
        in_specs=[SMEM] + [VMEM] * 4,
        out_specs=VMEM,
        scratch_shapes=[pltpu.VMEM((2, B // 2, NP * KB), BF)],
        compiler_params=limit(20),
        cost_estimate=cost(NP * 2 * B * B * K, 4),
    )(scalars, source, left, right, partial)


def pair_order(sect):
    core = sect & 1
    return 1 + 2 * core, 3 - 2 * core


def x_partner(step):
    return lambda x, z, sect: (x ^ pair_order(sect)[step], z)


def z_neighbour(x, z, sect):
    return (x, z ^ 1) if sect & 1 == 0 else (x, (z + 1 if z & 1 else z - 1) % 8)


def corner(x, z, sect):
    return x_partner(1)(*z_neighbour(x, z, sect), sect)


def z_group(mask):
    return lambda x, z, sect: (x, z ^ (2 * mask))


def swap(value, partner):
    sects = lax.axis_size("sect")
    moves = []
    for index in range(lax.axis_size("pairs")):
        for sect in range(sects):
            x, z = partner(index & 3, index >> 2, sect)
            moves.append((index * sects + sect, (z * 4 + x) * sects + sect))
    return lax.ppermute(value, ("pairs", "sect"), moves)


def local(
    wavefunction,
    left_normal,
    left_comp,
    right_comp,
    right_normal,
    pair_shift,
    pair_count,
    sector_rows,
):
    sects = lax.axis_size("sect")
    (
        wavefunction,
        left_normal,
        left_comp,
        right_comp,
        right_normal,
        pair_shift,
        sector_rows,
    ) = (
        pltpu.with_memory_space_constraint(value, pltpu.HBM)
        for value in (
            wavefunction,
            left_normal,
            left_comp.reshape(NP, 2, 16, ROW, B),
            right_comp,
            right_normal,
            pair_shift,
            sector_rows,
        )
    )
    last = mask_last(sector_rows, wavefunction)
    lower = lax.ppermute(last, "sect", [(i, i + 1) for i in range(sects - 1)])
    keep_b, send_b, scalars, mask_a, left_na, left_ca, right = upper_call(
        pair_count,
        pair_shift,
        sector_rows,
        last,
        wavefunction,
        left_normal,
        left_comp,
        right_comp,
        right_normal,
    )
    part_a = lower_normal(scalars, mask_a, left_na, right)
    comp = (scalars, lower, left_ca, right, part_a)
    send_a = lower_comp("lower_send", (2, 3), BF, *comp)
    keep_a = lower_comp("lower_keep", (0, 1), F32, *comp)

    got_b = swap(send_b, x_partner(0))
    got_a = swap(send_a, x_partner(0))
    got_b, keep_a = lax.optimization_barrier((got_b, keep_a))
    sum_b = keep_b + got_b.astype(F32)
    got_b = swap(sum_b[:, 2:].astype(BF), z_neighbour)
    sum_a = keep_a + got_a.astype(F32)
    across = sum_a[1, 2:].astype(BF)
    across, got_b = lax.optimization_barrier((across, got_b))
    sum_b = sum_b[:, :2] + got_b.astype(F32)
    beside = jnp.concatenate([sum_a[1, :2], sum_b[1]]).astype(BF)
    got_beside = swap(beside, x_partner(1))
    got_across = swap(across, corner)
    got_along = swap(sum_a[0, 2:].astype(BF), z_neighbour)
    got_beside, got_across, got_along = lax.optimization_barrier(
        (got_beside, got_across, got_along)
    )
    sum_a = sum_a[0, :2] + got_along.astype(F32) + got_across.astype(F32)
    kept = jnp.concatenate([sum_a, sum_b[0]]) + got_beside.astype(F32)

    index = lax.axis_index("pairs")
    group = index >> 3

    def pick(value, at):
        return lax.dynamic_index_in_dim(value, at, 0, keepdims=False)

    own = pick(kept, group)
    for mask in (2, 3, 1):
        got = swap(pick(kept, group ^ mask).astype(BF), z_group(mask))
        if mask == 2:
            got, scalars = lax.optimization_barrier((got, scalars))
        own = own + got.astype(F32)
    used = lax.dynamic_index_in_dim(scalars, ROWS + (group >> 1), 0)
    row = (index & 15) * ROW + lax.broadcasted_iota(jnp.int32, (ROW, K), 0)
    return jnp.where(row < used[None, :], own, jnp.zeros((), F32)).astype(BF)


def solution(mesh):
    placed = (
        P("sect", None),
        P("pairs", "sect", None, None),
        P("pairs", "sect", None, None),
        P("pairs", None, None, None),
        P("pairs", None, None, None),
        P("pairs"),
        P("pairs"),
        P("sect"),
    )
    return jax.shard_map(
        local, mesh=mesh, in_specs=placed, out_specs=P(("sect", "pairs"), None), check_vma=False
    )
```

```python
import jax
import jax.numpy as jnp
from jax import lax
from jax.experimental import pallas as pl
from jax.experimental.pallas import tpu as pltpu
from jax.sharding import PartitionSpec as P

B = 512
KB = 512
K = 1024
NP = 2
ROW = 32
SHIFT, ROWS, LIVE = 0, 2, 4
BF = jnp.bfloat16
F32 = jnp.float32
ANY = pl.BlockSpec(memory_space=pl.ANY)
HBM = pl.BlockSpec(memory_space=pltpu.HBM)
SMEM = pl.BlockSpec(memory_space=pltpu.SMEM)
VMEM = pl.BlockSpec(memory_space=pltpu.VMEM)


NT = (((1,), (1,)), ((), ()))


def masked_rows(value, first_row, used):
    at = lax.broadcasted_iota(jnp.int32, value.shape, 0) + first_row
    return jnp.where(at < used, value, jnp.zeros((), BF))


def for_live(live, act):
    for pairs in range(1, NP + 1):

        @pl.when(live == pairs)
        def _():
            act(pairs)


def left_product(left, source, inner, shift, pairs, terms, term):
    out = jnp.dot(left, source[...], preferred_element_type=F32).astype(BF)
    rows = out.shape[0] // pairs
    for p in range(pairs):
        for half in range(2):
            at = (p * terms + term) * KB
            inner[(half + shift[p]) & 1, :, at : at + KB] = out[
                p * rows : (p + 1) * rows, half * KB : (half + 1) * KB
            ]


def row_groups(places):
    index = lax.axis_index("pairs")
    my_x, parity = index & 3, (index >> 2) & 1
    first, second = pair_order(lax.axis_index("sect"))
    rels = (0, second, first, 2)
    return [
        (2 * (zplace % 2) + (parity ^ (zplace // 2))) * 4 + (my_x ^ rels[place])
        for place in places
        for zplace in range(4)
    ]


def cost(flops, mib):
    return pl.CostEstimate(flops=flops, bytes_accessed=mib * 2**20, transcendentals=0)


def limit(mib):
    return pltpu.CompilerParams(vmem_limit_bytes=mib * 2**20)


def mask_last(sector_rows, wavefunction):
    chunk = B // 8

    def body(rows_ref, wave, out, buf, rows, sems):
        copies = [
            pltpu.make_async_copy(
                wave.at[pl.ds(B + c * chunk, chunk), :], buf.at[pl.ds(c * chunk, chunk), :], sems.at[c]
            )
            for c in range(8)
        ]
        count = pltpu.make_async_copy(rows_ref, rows, sems.at[8])
        count.start()
        for copy in copies:
            copy.start()
        count.wait()
        for c, copy in enumerate(copies):
            copy.wait()
            part = slice(c * chunk, (c + 1) * chunk)
            out[part, :] = masked_rows(buf[part, :], c * chunk, rows[1])

    return pl.pallas_call(
        body,
        name="mask_last",
        out_shape=jax.ShapeDtypeStruct((B, K), BF),
        in_specs=[HBM] * 2,
        out_specs=VMEM,
        scratch_shapes=[
            pltpu.VMEM((B, K), BF),
            pltpu.SMEM((2,), jnp.int32),
            pltpu.SemaphoreType.DMA((9,)),
        ],
        compiler_params=limit(8),
        cost_estimate=cost(B * K, 2),
    )(sector_rows, wavefunction)


def upper_call(pair_count, pair_shift, sector_rows, mask_b, wavefunction, left_normal, left_comp, right_comp, right_normal):
    def body(
        cnt, shift_ref, rows_ref, m_b, wave, ln, lc, rc, rn,
        keep, send, scal, m_a, l_na, l_ca, right,
        raw, l_nb, l_cb, inner, acc, shift, rows, sems,
    ):
        wave_copy = pltpu.make_async_copy(wave.at[pl.ds(0, B), :], raw, sems.at[0])

        def left_copies(source, sector, target, size, sem):
            return [
                pltpu.make_async_copy(
                    source.at[p, sector], target.at[pl.ds(p * size, size)], sems.at[sem + p]
                )
                for p in range(NP)
            ]

        def right_copies(source, term, sem):
            return [
                pltpu.make_async_copy(
                    source.at[p], right.at[:, :, pl.ds((p * 2 + term) * KB, KB)], sems.at[sem + p]
                )
                for p in range(NP)
            ]

        normal_b = left_copies(ln, 1, l_nb, B, 1)
        comp_b = left_copies(lc, 1, l_cb, 16, 3)
        rights = right_copies(rc, 0, 5) + right_copies(rn, 1, 7)
        lower = left_copies(ln, 0, l_na, B, 9) + left_copies(lc, 0, l_ca, 16, 11)
        scalars = [
            pltpu.make_async_copy(shift_ref, shift, sems.at[13]),
            pltpu.make_async_copy(rows_ref, rows, sems.at[14]),
        ]
        for copy in scalars + normal_b + [wave_copy] + comp_b + rights:
            copy.start()
        for copy in scalars:
            copy.wait()
        for i in range(2):
            scal[SHIFT + i] = shift[i]
            scal[ROWS + i] = rows[i]
        scal[LIVE] = cnt[0]
        for copy in normal_b:
            copy.wait()
        for_live(
            cnt[0], lambda pairs: left_product(l_nb[: pairs * B, :], m_b, inner, shift, pairs, 2, 0)
        )
        for copy in lower:
            copy.start()
        wave_copy.wait()
        m_a[...] = masked_rows(raw[...], 0, rows[0])
        for copy in comp_b:
            copy.wait()
        for_live(
            cnt[0],
            lambda pairs: left_product(
                l_cb[: pairs * 16].reshape(pairs * B, B), m_a, inner, shift, pairs, 2, 1
            ),
        )
        for copy in rights:
            copy.wait()

        def finish(pairs):
            for j in range(2):
                acc[j] = lax.dot_general(
                    inner[j, :, : 2 * pairs * KB],
                    right[j, :, : 2 * pairs * KB],
                    NT,
                    preferred_element_type=F32,
                ).reshape(16, ROW, KB)

        for_live(cnt[0], finish)
        for i, group in enumerate(row_groups(range(4))):
            for j in range(2):
                cols = slice(j * KB, (j + 1) * KB)
                value = acc[j, group]
                if i < 8:
                    keep[i // 4, i % 4, :, cols] = value
                else:
                    send[i // 4 - 2, i % 4, :, cols] = value.astype(BF)
        for copy in lower:
            copy.wait()

    return pl.pallas_call(
        body,
        name="upper",
        out_shape=(
            jax.ShapeDtypeStruct((2, 4, ROW, K), F32),
            jax.ShapeDtypeStruct((2, 4, ROW, K), BF),
            jax.ShapeDtypeStruct((8,), jnp.int32),
            jax.ShapeDtypeStruct((B, K), BF),
            jax.ShapeDtypeStruct((NP * B, B), BF),
            jax.ShapeDtypeStruct((NP * 16, ROW, B), BF),
            jax.ShapeDtypeStruct((2, KB, 2 * NP * KB), BF),
        ),
        in_specs=[SMEM, HBM, HBM, VMEM] + [HBM] * 5,
        out_specs=(VMEM, VMEM, SMEM) + (VMEM,) * 4,
        scratch_shapes=[
            pltpu.VMEM((B, K), BF),
            pltpu.VMEM((NP * B, B), BF),
            pltpu.VMEM((NP * 16, ROW, B), BF),
            pltpu.VMEM((2, B, 2 * NP * KB), BF),
            pltpu.VMEM((2, 16, ROW, KB), F32),
            pltpu.SMEM((2,), jnp.int32),
            pltpu.SMEM((2,), jnp.int32),
            pltpu.SemaphoreType.DMA((15,)),
        ],
        compiler_params=limit(20),
        cost_estimate=cost(2 * NP * 4 * B * B * K, 10),
    )(
        pair_count,
        pair_shift,
        sector_rows,
        mask_b,
        wavefunction,
        left_normal,
        left_comp,
        right_comp,
        right_normal,
    )


def right_product(inner, right, j, term, pairs):
    ops = [right[j, :, (p * 2 + term) * KB : (p * 2 + term + 1) * KB] for p in range(pairs)]
    return lax.dot_general(
        inner[j, :, : pairs * KB],
        jnp.concatenate(ops, axis=1) if pairs > 1 else ops[0],
        NT,
        preferred_element_type=F32,
    )


def lower_normal(scalars, source, left, right):
    def body(scal, src, lft, rgt, out, inner):
        def act(pairs):
            left_product(lft[: pairs * B, :], src, inner, scal, pairs, 1, 0)
            for j in range(2):
                out[j] = right_product(inner, rgt, j, 0, pairs).reshape(16, ROW, KB)

        for_live(scal[LIVE], act)

    return pl.pallas_call(
        body,
        name="lower_normal",
        out_shape=jax.ShapeDtypeStruct((2, 16, ROW, KB), F32),
        in_specs=[SMEM] + [VMEM] * 3,
        out_specs=VMEM,
        scratch_shapes=[pltpu.VMEM((2, B, NP * KB), BF)],
        compiler_params=limit(20),
        cost_estimate=cost(NP * 4 * B * B * K, 4),
    )(scalars, source, left, right)


def lower_comp(name, places, dtype, scalars, source, left, right, partial):
    def body(scal, src, lft, rgt, part, out, inner):
        groups = row_groups(places)

        def act(pairs):
            rows = [lft[p * 16 + group] for p in range(pairs) for group in groups]
            left_product(jnp.concatenate(rows, axis=0), src, inner, scal, pairs, 1, 0)
            for j in range(2):
                cols = slice(j * KB, (j + 1) * KB)
                total = right_product(inner, rgt, j, 1, pairs).reshape(8, ROW, KB)
                for i, group in enumerate(groups):
                    out[i // 4, i % 4, :, cols] = (part[j, group] + total[i]).astype(dtype)

        for_live(scal[LIVE], act)

    return pl.pallas_call(
        body,
        name=name,
        out_shape=jax.ShapeDtypeStruct((2, 4, ROW, K), dtype),
        in_specs=[SMEM] + [VMEM] * 4,
        out_specs=VMEM,
        scratch_shapes=[pltpu.VMEM((2, B // 2, NP * KB), BF)],
        compiler_params=limit(20),
        cost_estimate=cost(NP * 2 * B * B * K, 4),
    )(scalars, source, left, right, partial)


def pair_order(sect):
    core = sect & 1
    return 1 + 2 * core, 3 - 2 * core


def x_partner(step):
    return lambda x, z, sect: (x ^ pair_order(sect)[step], z)


def z_neighbour(x, z, sect):
    return (x, z ^ 1) if sect & 1 == 0 else (x, (z + 1 if z & 1 else z - 1) % 8)


def corner(x, z, sect):
    return x_partner(1)(*z_neighbour(x, z, sect), sect)


def z_group(mask):
    return lambda x, z, sect: (x, z ^ (2 * mask))


def swap(value, partner):
    sects = lax.axis_size("sect")
    moves = []
    for index in range(lax.axis_size("pairs")):
        for sect in range(sects):
            x, z = partner(index & 3, index >> 2, sect)
            moves.append((index * sects + sect, (z * 4 + x) * sects + sect))
    return lax.ppermute(value, ("pairs", "sect"), moves)


def local(
    wavefunction,
    left_normal,
    left_comp,
    right_comp,
    right_normal,
    pair_shift,
    pair_count,
    sector_rows,
):
    sects = lax.axis_size("sect")
    (
        wavefunction,
        left_normal,
        left_comp,
        right_comp,
        right_normal,
        pair_shift,
        sector_rows,
    ) = (
        pltpu.with_memory_space_constraint(value, pltpu.HBM)
        for value in (
            wavefunction,
            left_normal,
            left_comp.reshape(NP, 2, 16, ROW, B),
            right_comp,
            right_normal,
            pair_shift,
            sector_rows,
        )
    )
    last = mask_last(sector_rows, wavefunction)
    lower = lax.ppermute(last, "sect", [(i, i + 1) for i in range(sects - 1)])
    keep_b, send_b, scalars, mask_a, left_na, left_ca, right = upper_call(
        pair_count,
        pair_shift,
        sector_rows,
        last,
        wavefunction,
        left_normal,
        left_comp,
        right_comp,
        right_normal,
    )
    part_a = lower_normal(scalars, mask_a, left_na, right)
    comp = (scalars, lower, left_ca, right, part_a)
    send_a = lower_comp("lower_send", (2, 3), BF, *comp)
    keep_a = lower_comp("lower_keep", (0, 1), F32, *comp)

    got_b = swap(send_b, x_partner(0))
    got_a = swap(send_a, x_partner(0))
    got_b, keep_a = lax.optimization_barrier((got_b, keep_a))
    sum_b = keep_b + got_b.astype(F32)
    got_b = swap(sum_b[:, 2:].astype(BF), z_neighbour)
    sum_a = keep_a + got_a.astype(F32)
    across = sum_a[1, 2:].astype(BF)
    across, got_b = lax.optimization_barrier((across, got_b))
    sum_b = sum_b[:, :2] + got_b.astype(F32)
    beside = jnp.concatenate([sum_a[1, :2], sum_b[1]]).astype(BF)
    got_beside = swap(beside, x_partner(1))
    got_across = swap(across, corner)
    got_along = swap(sum_a[0, 2:].astype(BF), z_neighbour)
    got_beside, got_across, got_along = lax.optimization_barrier(
        (got_beside, got_across, got_along)
    )
    sum_a = sum_a[0, :2] + got_along.astype(F32) + got_across.astype(F32)
    kept = jnp.concatenate([sum_a, sum_b[0]]) + got_beside.astype(F32)

    index = lax.axis_index("pairs")
    group = index >> 3

    def pick(value, at):
        return lax.dynamic_index_in_dim(value, at, 0, keepdims=False)

    own = pick(kept, group)
    for mask in (2, 3, 1):
        got = swap(pick(kept, group ^ mask).astype(BF), z_group(mask))
        if mask == 2:
            got, scalars = lax.optimization_barrier((got, scalars))
        own = own + got.astype(F32)
    used = lax.dynamic_index_in_dim(scalars, ROWS + (group >> 1), 0)
    row = (index & 15) * ROW + lax.broadcasted_iota(jnp.int32, (ROW, K), 0)
    return jnp.where(row < used[None, :], own, jnp.zeros((), F32)).astype(BF)


def solution(mesh):
    placed = (
        P("sect", None),
        P("pairs", "sect", None, None),
        P("pairs", "sect", None, None),
        P("pairs", None, None, None),
        P("pairs", None, None, None),
        P("pairs"),
        P("pairs"),
        P("sect"),
    )
    return jax.shard_map(
        local, mesh=mesh, in_specs=placed, out_specs=P(("sect", "pairs"), None), check_vma=False
    )
```
